512 devices in a mesh: prow: 32 (over y, x), pcol: 8 (over z), zgrid: 2 (over core).
Axes of the slice: x: 4, y: 8, z: 8, core: 2. Of those that a mesh axis runs over, the one named last changes fastest.
Arguments:
- blocks: bfloat16 [32, 8, 2, 3, 40, 128, 128], P('prow', 'pcol', 'zgrid'), may hold values from -0.078125 to 0.078125
- sources: int32 [32, 8, 2, 3, 40], P('prow', 'pcol', 'zgrid'), may hold values from 0 to 7, as said below
- targets: int32 [32, 8, 2, 3, 40], P('prow', 'pcol', 'zgrid'), may hold values from 0 to 95, as said below
- counts: int32 [32, 8, 2, 3], P('prow', 'pcol', 'zgrid'), may hold values from 1 to 40, as said below
- given_sub: bfloat16 [32, 8, 2, 2, 128, 128], P('prow', 'pcol', 'zgrid'), may hold values from -6 to 6
- given_top: bfloat16 [32, 8, 2, 128, 128], P('prow', 'pcol'), may hold values from -6 to 6
- inverse_sub: bfloat16 [32, 8, 2, 2, 128, 128], P('prow', 'pcol', 'zgrid'), as said below
- inverse_top: bfloat16 [32, 8, 2, 128, 128], P('prow', 'pcol'), as said below
Outputs:
- solved_sub: bfloat16 [32, 8, 2, 2, 128, 128], P('prow', 'pcol', 'zgrid')
- solved_top: bfloat16 [32, 8, 2, 128, 128], P('prow', 'pcol')
The draws below stay inside these ranges and needn't reach their ends.
Inputs may be any that keep to these rules, and one draw needn't show every extreme that they name: `sources`: column of the source supernode of a slot. `targets`: a slot of source level l aims at a level t = value // 32 + 1 above l and the row value % 32. `counts`: on some device of each source level all 40 slots are live. `inverse_sub`: unit lower triangular. `inverse_top`: unit lower triangular.
All inputs are finite; a program needn't handle non-finite values.
Results may differ from the reference program's by a relative error of at most 0.023.
Values may be sent and summed in bfloat16 or wider, within the bound.
A program may use at most 64 MiB of HBM per device.

```python
import math
import jax
import jax.numpy as jnp
from jax import lax

WIDTH = 128
SIDES = 128
CAP = 40
ROWS = 32
COLS = 8
LAYERS = 2


def draw_sources(key, part):
    return jax.random.randint(jax.random.fold_in(key, 101), (ROWS, COLS, LAYERS, 3, CAP), 0, COLS).astype(jnp.int32)


def draw_targets(key, part):
    first_key = jax.random.fold_in(key, 202)
    second_key = jax.random.fold_in(key, 203)
    shape_all = (ROWS, COLS, LAYERS, 3, CAP)
    lowest = jnp.arange(3, dtype=jnp.int32)[None, None, None, :, None] + 1
    level_pick = jax.random.randint(first_key, shape_all, lowest, 4)
    row_pick = jax.random.randint(second_key, shape_all, 0, ROWS)
    return ((level_pick - 1) * ROWS + row_pick).astype(jnp.int32)


def draw_counts(key, part):
    first_key = jax.random.fold_in(key, 301)
    second_key = jax.random.fold_in(key, 302)
    third_key = jax.random.fold_in(key, 303)
    devices_all = ROWS * COLS * LAYERS
    first_pick = jax.random.randint(first_key, (devices_all, 3), 1, CAP + 1)
    second_pick = jax.random.randint(second_key, (devices_all, 3), 1, CAP + 1)
    smaller = jnp.minimum(first_pick, second_pick)
    spots = jax.random.randint(third_key, (3,), 0, devices_all)
    smaller = smaller.at[spots, jnp.arange(3)].set(CAP)
    return smaller.reshape(ROWS, COLS, LAYERS, 3).astype(jnp.int32)


def unit_lower(key, shape_all):
    normal_part = jax.random.normal(key, shape_all, jnp.float32)
    lower_part = jnp.tril(normal_part, -1) * (0.5 / math.sqrt(WIDTH)) + jnp.eye(WIDTH, dtype=jnp.float32)
    return lower_part.astype(jnp.bfloat16)


def draw_inverse_sub(key, part):
    return unit_lower(jax.random.fold_in(key, 401), (ROWS, COLS, LAYERS, 2, WIDTH, WIDTH))


def draw_inverse_top(key, part):
    return unit_lower(jax.random.fold_in(key, 402), (ROWS, COLS, 2, WIDTH, WIDTH))


def level_of(own_key, shape, shards, smallest, high):
    loudness = 1.0
    for position, blocks in shards:
        heights = jax.random.uniform(jax.random.fold_in(jax.random.fold_in(own_key, 6), position), (blocks,), jnp.float32, smallest / len(shards), high / len(shards))
        loudness = loudness * jnp.repeat(jnp.exp(heights), shape[position] // blocks).reshape((-1,) + (1,) * (len(shape) - 1 - position))
    return loudness


def centred(stream_key, extent, spread, most, split=(), kind=jnp.bfloat16):
    array = spread * jax.random.normal(stream_key, extent, jnp.float32)
    if split:
        array = array * level_of(stream_key, extent, split, -0.22, 0.18)
    return jnp.clip(array, -most, most).astype(kind)


def setup_inputs(seed: int = 0) -> dict:
    key_of = jax.random.split(jax.random.key(seed), 9)
    return {
        "blocks": centred(key_of[0], (ROWS, COLS, LAYERS, 3, CAP, WIDTH, WIDTH), (WIDTH * CAP) ** -0.5, 0.078125, ((0, 32), (1, 8), (2, 2))),
        "sources": draw_sources(jax.random.fold_in(key_of[8], 71), 0),
        "targets": draw_targets(jax.random.fold_in(key_of[8], 71), 0),
        "counts": draw_counts(jax.random.fold_in(key_of[8], 71), 0),
        "given_sub": centred(key_of[4], (ROWS, COLS, LAYERS, 2, WIDTH, SIDES), 1.0, 6.0, ((0, 32), (1, 8), (2, 2))),
        "given_top": centred(key_of[5], (ROWS, COLS, 2, WIDTH, SIDES), 1.0, 6.0, ((0, 32), (1, 8))),
        "inverse_sub": draw_inverse_sub(jax.random.fold_in(key_of[8], 71), 0),
        "inverse_top": draw_inverse_top(jax.random.fold_in(key_of[8], 71), 0),
    }


def solve_block(inverse, residual):
    return jnp.einsum("...wk,...kr->...wr", inverse.astype(jnp.float32), residual.astype(jnp.float32)).astype(jnp.bfloat16)


def incoming_sums(target_level, blocks, sources, targets, counts, sub_now, top_now):
    row_count = blocks.shape[0]
    col_count = blocks.shape[1]
    layer_count = blocks.shape[2]
    slot_count = blocks.shape[4]
    width = blocks.shape[5]
    sides = sub_now.shape[-1]
    start_sum = jnp.zeros((col_count, layer_count, row_count, width, sides), jnp.float32)

    def row_step(carry, inputs):
        block_row, source_row, target_row, count_row, sub_row, top_row = inputs
        total = jnp.zeros((col_count, layer_count, row_count, width, sides), jnp.float32)
        layer_ids = jnp.arange(layer_count)[None, :, None]
        for source_level in range(target_level):
            source_part = source_row[:, :, source_level]
            target_part = target_row[:, :, source_level]
            if source_level < 2:
                chosen = sub_row[source_part, layer_ids, source_level]
            else:
                chosen = top_row[source_part]
            product = jnp.einsum("qzswk,qzskr->qzswr", block_row[:, :, source_level].astype(jnp.float32), chosen.astype(jnp.float32))
            alive_mask = (jnp.arange(slot_count)[None, None, :] < count_row[:, :, source_level][:, :, None]) & (target_part // row_count + 1 == target_level)
            one_hot = (((target_part % row_count)[..., None] == jnp.arange(row_count)) & alive_mask[..., None]).astype(jnp.float32)
            total = total + jnp.einsum("qzsp,qzswr->qzpwr", one_hot, product)
        rounded = lax.optimization_barrier(total.astype(jnp.bfloat16)).astype(jnp.float32)
        return carry + rounded, None

    result, unused = lax.scan(row_step, start_sum, (blocks, sources, targets, counts, sub_now, top_now))
    return result


def reference(blocks, sources, targets, counts, given_sub, given_top, inverse_sub, inverse_top):
    level_zero = solve_block(inverse_sub[:, :, :, 0], given_sub[:, :, :, 0])
    sub_now = jnp.stack([level_zero, jnp.zeros_like(level_zero)], axis=3)
    top_now = jnp.zeros(given_top[:, :, 0].shape, jnp.bfloat16)
    arrive_one = jnp.transpose(incoming_sums(1, blocks, sources, targets, counts, sub_now, top_now), (2, 0, 1, 3, 4))
    level_one = solve_block(inverse_sub[:, :, :, 1], (given_sub[:, :, :, 1].astype(jnp.float32) - arrive_one).astype(jnp.bfloat16))
    sub_now = jnp.stack([level_zero, level_one], axis=3)
    arrive_two = jnp.transpose(jnp.sum(incoming_sums(2, blocks, sources, targets, counts, sub_now, top_now), axis=1), (1, 0, 2, 3))
    level_two = solve_block(inverse_top[:, :, 0], (given_top[:, :, 0].astype(jnp.float32) - arrive_two).astype(jnp.bfloat16))
    arrive_three = jnp.transpose(jnp.sum(incoming_sums(3, blocks, sources, targets, counts, sub_now, level_two), axis=1), (1, 0, 2, 3))
    level_three = solve_block(inverse_top[:, :, 1], (given_top[:, :, 1].astype(jnp.float32) - arrive_three).astype(jnp.bfloat16))
    return sub_now, jnp.stack([level_two, level_three], axis=2)
```

```python
import functools

import jax
import jax.numpy as jnp
from jax import lax
from jax.experimental import pallas as pl
from jax.experimental.pallas import tpu as pltpu
from jax.sharding import PartitionSpec as P

MESH = pl.DeviceIdType.MESH
X_CHIPS = 4


def index_table(sources, targets, counts, rows):
    levels, cap = targets.shape
    slots = levels * cap
    order = jnp.arange(slots, dtype=jnp.int32)
    live = (order % cap) < jnp.repeat(counts, cap)
    key = jnp.where(live, targets.reshape(-1), -1)
    wanted = jnp.concatenate(
        [jnp.where(live, key, -2), jnp.arange(levels * rows, dtype=jnp.int32)]
    )
    limit = jnp.concatenate(
        [order, jnp.repeat((jnp.arange(levels, dtype=jnp.int32) + 1) * cap, rows)]
    )
    hit = (wanted[:, None] == key[None, :]) & (order[None, :] < limit[:, None])
    found = jnp.max(jnp.where(hit, order[None, :], -1), axis=1)
    found = jnp.where(found < 0, slots, found)
    return jnp.concatenate([sources.reshape(-1), found])


def drain(ref, sem):
    pltpu.make_async_copy(ref, ref, sem).wait()


def kernel(
    sizes, table, blocks, given_sub, given_top, inverse_sub, inverse_top,
    out_sub, out_top,
    block_v, given_v, inverse_v, run, gathered_0, gathered_1, gathered_2,
    sums_1, xa_1, ya_in_1, ya_1, yb_1, xb_in_1, xb_1,
    give_t, take_t, sums_t, xa_t, ya_in_t, ya_t, yb_t, xb_in_t, xb_t, half_t, other_t,
    load_sem, small_sem, send_sem, recv_sem,
):
    nx, ny, nc, cap, width, sides, cut_1, cut_t = sizes
    rows = nx * ny
    half = width // 2
    slots = 3 * cap
    gathered = (gathered_0, gathered_1, gathered_2)
    p = lax.axis_index("prow")
    c = lax.axis_index("pcol")
    k = lax.axis_index("zgrid")
    x = lax.rem(p, nx)
    y = lax.div(p, nx)

    def x_peer(d):
        return {"prow": y * nx + lax.rem(x + d, nx)}

    def y_peer(d):
        return {"prow": lax.rem(y + d, ny) * nx + x}

    def z_peer(d):
        return {"pcol": lax.rem(c + d, nc)}

    core = {"zgrid": 1 - k}
    x_order = [d for d in (2, 1, nx - 1) if 0 < d < nx][: nx - 1]
    x_order = list(dict.fromkeys(x_order))
    y_order = sorted(range(1, ny), key=lambda d: -min(d, ny - d))
    z_order = sorted(range(1, nc), key=lambda d: -min(d, nc - d))

    def send(src, dst, slot, device):
        pltpu.make_async_remote_copy(
            src_ref=src, dst_ref=dst, send_sem=send_sem.at[slot], recv_sem=recv_sem.at[slot],
            device_id=device, device_id_type=MESH,
        ).start()

    loads = [pltpu.make_async_copy(blocks.at[l], block_v.at[l], load_sem.at[l]) for l in range(3)]
    smalls = []
    for j in range(4):
        g = given_sub.at[j] if j < 2 else given_top.at[j - 2]
        i = inverse_sub.at[j] if j < 2 else inverse_top.at[j - 2]
        smalls.append(pltpu.make_async_copy(g, given_v.at[j], small_sem.at[2 * j]))
        smalls.append(pltpu.make_async_copy(i, inverse_v.at[j], small_sem.at[2 * j + 1]))
    for s in smalls[:2]:
        s.start()
    loads[0].start()
    for s in smalls[2:]:
        s.start()
    loads[1].start()
    loads[2].start()

    barrier = pltpu.get_barrier_semaphore()
    partners = (
        [x_peer(d) for d in x_order] + [y_peer(d) for d in y_order]
        + [z_peer(d) for d in z_order] + [core]
    )
    for device in partners:
        pl.semaphore_signal(barrier, inc=1, device_id=device, device_id_type=MESH)

    run[slots] = jnp.zeros((width, sides), jnp.float32)
    for s in smalls:
        s.wait()

    def solve(l, residual):
        return jnp.dot(
            inverse_v[l], residual, preferred_element_type=jnp.float32
        ).astype(jnp.bfloat16)

    def share(l, solved):
        held = gathered[l]
        held[c] = solved
        for d in z_order:
            send(held.at[c], held.at[c], l, z_peer(d))

    def products(l):
        held = gathered[l]
        drain(held.at[pl.ds(0, nc - 1)], recv_sem.at[l])
        loads[l].wait()
        group = 4

        def step(i, carry):
            base = i * group
            values = [
                jnp.dot(
                    block_v[l, base + u], held[table[l * cap + base + u]],
                    preferred_element_type=jnp.float32,
                )
                for u in range(group)
            ]
            for u in range(group):
                s = l * cap + base + u
                run[s] = values[u] + run[table[slots + s]]
            return carry

        lax.fori_loop(0, cap // group, step, 0)

    def total(l, row):
        return run[table[2 * slots + l * rows + row]]

    def reduce_rows(sums, height, cut, xa, ya_in, ya, yb, xb_in, xb, base):
        low = pl.ds(0, cut)
        high = pl.ds(cut, height - cut)
        for d in x_order:
            to = lax.rem(x + d, nx)
            send(sums.at[to, :, low], xa.at[d - 1], base, x_peer(d))
        for d in y_order:
            to = lax.rem(y + d, ny)
            send(sums.at[:, to, high], yb.at[d - 1], base + 1, y_peer(d))
        drain(xa, recv_sem.at[base])

        def add_x(j, carry):
            value = sums[x, j, low].astype(jnp.float32)
            for d in range(nx - 1):
                value = value + xa[d, j].astype(jnp.float32)
            ya_in[j] = value.astype(jnp.bfloat16)
            return carry

        lax.fori_loop(0, ny, add_x, 0)
        for d in y_order:
            send(ya_in.at[lax.rem(y + d, ny)], ya.at[d - 1], base + 2, y_peer(d))
        drain(yb, recv_sem.at[base + 1])

        def add_y(j, carry):
            value = sums[j, y, high].astype(jnp.float32)
            for d in range(ny - 1):
                value = value + yb[d, j].astype(jnp.float32)
            xb_in[j] = value.astype(jnp.bfloat16)
            return carry

        lax.fori_loop(0, nx, add_y, 0)
        for d in x_order:
            send(xb_in.at[lax.rem(x + d, nx)], xb.at[d - 1], base + 3, x_peer(d))
        drain(xb, recv_sem.at[base + 3])
        upper = xb_in[x].astype(jnp.float32)
        for d in range(nx - 1):
            upper = upper + xb[d].astype(jnp.float32)
        drain(ya, recv_sem.at[base + 2])
        lower = ya_in[y].astype(jnp.float32)
        for d in range(ny - 1):
            lower = lower + ya[d].astype(jnp.float32)
        return lower, upper

    pl.semaphore_wait(barrier, len(partners))

    level_zero = solve(0, given_v[0])
    share(0, level_zero)
    out_sub[0] = level_zero
    products(0)

    def place_1(j, carry):
        sums_1[lax.rem(j, nx), lax.div(j, nx)] = total(0, j).astype(jnp.bfloat16)
        return carry

    lax.fori_loop(0, rows, place_1, 0)
    lower, upper = reduce_rows(sums_1, width, cut_1, xa_1, ya_in_1, ya_1, yb_1, xb_in_1, xb_1, 3)
    incoming = jnp.concatenate([lower, upper], axis=0)
    level_one = solve(1, (given_v[1].astype(jnp.float32) - incoming).astype(jnp.bfloat16))
    share(1, level_one)
    out_sub[1] = level_one
    products(1)

    mine = pl.ds(pl.multiple_of(k * half, half), half)
    theirs = pl.ds(pl.multiple_of((1 - k) * half, half), half)

    def ancestor(l):
        t = l - 1
        base = 7 + 6 * t

        def place(j, carry):
            give_t[t, lax.rem(j, nx), lax.div(j, nx)] = run[
                table[2 * slots + l * rows + j], theirs
            ].astype(jnp.bfloat16)
            return carry

        lax.fori_loop(0, rows, place, 0)
        send(give_t.at[t], take_t.at[t], base, core)
        drain(take_t.at[t], recv_sem.at[base])

        def merge(j, carry):
            i, m = lax.rem(j, nx), lax.div(j, nx)
            value = run[table[2 * slots + l * rows + j], mine]
            sums_t[t, i, m] = (value + take_t[t, i, m].astype(jnp.float32)).astype(jnp.bfloat16)
            return carry

        lax.fori_loop(0, rows, merge, 0)
        lower, upper = reduce_rows(
            sums_t.at[t], half, cut_t, xa_t.at[t], ya_in_t.at[t], ya_t.at[t],
            yb_t.at[t], xb_in_t.at[t], xb_t.at[t], base + 1,
        )
        incoming = jnp.concatenate([lower, upper], axis=0)
        residual = given_v[l + 1, mine].astype(jnp.float32) - incoming
        half_t[t, mine] = residual.astype(jnp.bfloat16)
        send(half_t.at[t, mine], other_t.at[t], base + 5, core)
        drain(other_t.at[t], recv_sem.at[base + 5])
        half_t[t, theirs] = other_t[t]
        return solve(l + 1, half_t[t])

    level_two = ancestor(1)
    share(2, level_two)
    out_top[0] = level_two
    products(2)
    level_three = ancestor(2)
    out_top[1] = level_three

    for l in range(3):
        drain(gathered[l].at[pl.ds(0, nc - 1)], send_sem.at[l])
    for refs, base in (
        ((xa_1, yb_1, ya_1, xb_1), 3),
        ((take_t.at[0], xa_t.at[0], yb_t.at[0], ya_t.at[0], xb_t.at[0], other_t.at[0]), 7),
        ((take_t.at[1], xa_t.at[1], yb_t.at[1], ya_t.at[1], xb_t.at[1], other_t.at[1]), 13),
    ):
        for j, ref in enumerate(refs):
            drain(ref, send_sem.at[base + j])


def local(nx, axis_sizes, blocks, sources, targets, counts, given_sub, given_top, inverse_sub, inverse_top):
    rows, nc = axis_sizes
    ny = rows // nx
    levels, cap, width = blocks.shape[3:6]
    sides = given_sub.shape[-1]
    half = width // 2
    cut_1 = width * 3 // 4
    cut_t = half * 3 // 4
    table = index_table(sources[0, 0, 0], targets[0, 0, 0], counts[0, 0, 0], rows)
    sizes = (nx, ny, nc, cap, width, sides, cut_1, cut_t)
    bf16 = jnp.bfloat16

    def exchange(lead, height, cut):
        rest = height - cut
        return [
            pltpu.VMEM(lead + (nx - 1, ny, cut, sides), bf16),
            pltpu.VMEM(lead + (ny, cut, sides), bf16),
            pltpu.VMEM(lead + (ny - 1, cut, sides), bf16),
            pltpu.VMEM(lead + (ny - 1, nx, rest, sides), bf16),
            pltpu.VMEM(lead + (nx, rest, sides), bf16),
            pltpu.VMEM(lead + (nx - 1, rest, sides), bf16),
        ]

    anywhere = pl.BlockSpec(memory_space=pltpu.HBM)
    vmem = pl.BlockSpec(memory_space=pltpu.VMEM)
    solved_sub, solved_top = pl.pallas_call(
        functools.partial(kernel, sizes),
        out_shape=(
            jax.ShapeDtypeStruct((2, width, sides), bf16),
            jax.ShapeDtypeStruct((2, width, sides), bf16),
        ),
        in_specs=[pl.BlockSpec(memory_space=pltpu.SMEM)] + [anywhere] * 5,
        out_specs=(vmem, vmem),
        scratch_shapes=[
            pltpu.VMEM((levels, cap, width, width), bf16),
            pltpu.VMEM((4, width, sides), bf16),
            pltpu.VMEM((4, width, width), bf16),
            pltpu.VMEM((levels * cap + 1, width, sides), jnp.float32),
            pltpu.VMEM((nc, width, sides), bf16),
            pltpu.VMEM((nc, width, sides), bf16),
            pltpu.VMEM((nc, width, sides), bf16),
            pltpu.VMEM((nx, ny, width, sides), bf16),
            *exchange((), width, cut_1),
            pltpu.VMEM((2, nx, ny, half, sides), bf16),
            pltpu.VMEM((2, nx, ny, half, sides), bf16),
            pltpu.VMEM((2, nx, ny, half, sides), bf16),
            *exchange((2,), half, cut_t),
            pltpu.VMEM((2, width, sides), bf16),
            pltpu.VMEM((2, half, sides), bf16),
            pltpu.SemaphoreType.DMA((3,)),
            pltpu.SemaphoreType.DMA((8,)),
            pltpu.SemaphoreType.DMA((19,)),
            pltpu.SemaphoreType.DMA((19,)),
        ],
        compiler_params=pltpu.CompilerParams(
            collective_id=0, has_side_effects=True, vmem_limit_bytes=60 * 1024 * 1024
        ),
        name="substitution",
    )(
        table, blocks[0, 0, 0], given_sub[0, 0, 0], given_top[0, 0],
        inverse_sub[0, 0, 0], inverse_top[0, 0],
    )
    return solved_sub[None, None, None], solved_top[None, None]


def solution(mesh):
    nx = X_CHIPS
    in_specs = (
        P("prow", "pcol", "zgrid", None, None, None, None),
        P("prow", "pcol", "zgrid", None, None),
        P("prow", "pcol", "zgrid", None, None),
        P("prow", "pcol", "zgrid", None),
        P("prow", "pcol", "zgrid", None, None, None),
        P("prow", "pcol", None, None, None),
        P("prow", "pcol", "zgrid", None, None, None),
        P("prow", "pcol", None, None, None),
    )
    out_specs = (P("prow", "pcol", "zgrid", None, None, None), P("prow", "pcol", None, None, None))
    body = functools.partial(local, nx, (mesh.shape["prow"], mesh.shape["pcol"]))
    return jax.shard_map(body, mesh=mesh, in_specs=in_specs, out_specs=out_specs, check_vma=False)
```

```python
import functools

import jax
import jax.numpy as jnp
from jax import lax
from jax.experimental import pallas as pl
from jax.experimental.pallas import tpu as pltpu
from jax.sharding import PartitionSpec as P

MESH = pl.DeviceIdType.MESH
X_CHIPS = 4
PARTS = 2
LANES = 128
STEPS = ("g0", "x1", "y1", "g1", "c2", "x2", "y2", "g2", "f2", "c3", "x3", "y3", "f3")


def drain(ref, sem):
    pltpu.make_async_copy(ref, ref, sem).wait()


def times_transposed(left, right):
    return lax.dot_general(
        left, right, (((1,), (1,)), ((), ())), preferred_element_type=jnp.float32
    )


def kernel(
    sizes, sources, counts, targets, blocks, given_sub, given_top, inverse_sub, inverse_top,
    out_sub, out_top, key_v, table_v, table, block_v, given_v, given_t, inverse_v, run, top, *rest
):
    nx, ny, nc, cap, width, sides = sizes
    rows = nx * ny
    slots = 3 * cap
    part = sides // PARTS
    fine = part // 2
    gathered = [rest[PARTS * l : PARTS * (l + 1)] for l in range(3)]
    rest = rest[3 * PARTS :]
    sums, xa, y_in, ya = [[rest[4 * j + i] for j in range(3)] for i in range(4)]
    give, take, table_sem, load_sem, small_sem, send_sem, recv_sem = rest[12:]
    p = lax.axis_index("prow")
    c = lax.axis_index("pcol")
    k = lax.axis_index("zgrid")
    x = lax.rem(p, nx)
    y = lax.div(p, nx)

    def x_peer(d):
        return {"prow": y * nx + lax.rem(x + d, nx)}

    def y_peer(d):
        return {"prow": lax.rem(y + d, ny) * nx + x}

    def z_peer(d):
        return {"pcol": lax.rem(c + d, nc)}

    core = {"zgrid": 1 - k}
    x_order = sorted(range(1, nx), key=lambda d: -min(d, nx - d))
    y_order = sorted(range(1, ny), key=lambda d: -min(d, ny - d))
    z_order = sorted(range(1, nc), key=lambda d: -min(d, nc - d))
    pending = {}

    def sem_of(step, j):
        return STEPS.index(step) * PARTS + j

    def send(src, dst, step, j, device, everything):
        slot = sem_of(step, j)
        pending[slot] = everything
        pltpu.make_async_remote_copy(
            src_ref=src, dst_ref=dst, send_sem=send_sem.at[slot], recv_sem=recv_sem.at[slot],
            device_id=device, device_id_type=MESH,
        ).start()

    def arrive(step, j):
        slot = sem_of(step, j)
        drain(pending[slot], recv_sem.at[slot])

    def finish():
        for slot, everything in pending.items():
            drain(everything, send_sem.at[slot])

    loads = [pltpu.make_async_copy(blocks.at[l], block_v.at[l], load_sem.at[l]) for l in range(3)]
    smalls = []
    for n in range(4):
        g = given_sub.at[n] if n < 2 else given_top.at[n - 2]
        i = inverse_sub.at[n] if n < 2 else inverse_top.at[n - 2]
        smalls.append(pltpu.make_async_copy(g, given_v.at[n], small_sem.at[2 * n]))
        smalls.append(pltpu.make_async_copy(i, inverse_v.at[n], small_sem.at[2 * n + 1]))
    for s in smalls:
        s.start()
    for s in loads:
        s.start()

    barrier = pltpu.get_barrier_semaphore()
    partners = (
        [x_peer(d) for d in x_order] + [y_peer(d) for d in y_order]
        + [z_peer(d) for d in z_order] + [core]
    )
    for device in partners:
        pl.semaphore_signal(barrier, inc=1, device_id=device, device_id_type=MESH)

    lanes = lax.broadcasted_iota(jnp.int32, (1, LANES), 1)
    key_v[...] = jnp.full(key_v.shape, -1, jnp.int32)
    for l in range(3):
        live = lanes[:, :cap] < counts[0, l]
        key_v[l : l + 1, :cap] = jnp.where(live, targets[l], -1)
    key_rows = key_v[...]
    key_columns = key_rows.T
    line = lax.broadcasted_iota(jnp.int32, (LANES, LANES), 0)
    lane = lax.broadcasted_iota(jnp.int32, (LANES, LANES), 1)

    def latest(wanted, l, strict):
        best = jnp.full((1, LANES), -1, jnp.int32)
        for m in range(l + 1):
            hit = (key_columns[:, m : m + 1] == wanted) & (wanted >= 0)
            if m == l and strict:
                hit = hit & (line < lane)
            best = jnp.maximum(best, jnp.max(jnp.where(hit, line + m * cap, -1), axis=0, keepdims=True))
        return jnp.where(best < 0, slots, best)

    for l in range(3):
        table_v[l : l + 1] = latest(key_rows[l : l + 1], l, True)
        table_v[3 + l : 4 + l] = latest(lanes + l * rows, l, False)
    to_scalars = pltpu.make_async_copy(table_v, table, table_sem)
    to_scalars.start()
    run[slots] = jnp.zeros((sides, width), jnp.float32)
    for s in smalls:
        s.wait()
    for n in range(4):
        given_t[n] = given_v[n].astype(jnp.float32).T

    def natural(j, h):
        return pl.ds(h * part + j * fine, fine)

    def of_part(l, j):
        return jnp.concatenate([given_t[l, natural(j, h)] for h in range(2)], axis=0)

    def solve(l, residual):
        solved = times_transposed(residual.astype(jnp.bfloat16), inverse_v[l])
        return solved.astype(jnp.bfloat16)

    def share(l, j, solved):
        held = gathered[l][j]
        held[c] = solved
        for d in z_order:
            send(held.at[c], held.at[c], f"g{l}", j, z_peer(d), held.at[pl.ds(0, nc - 1)])

    def turn(l):
        loads[l].wait()

        def step(i, carry):
            for u in range(4):
                block_v[l, i * 4 + u] = block_v[l, i * 4 + u].T
            return carry

        lax.fori_loop(0, cap // 4, step, 0)

    def products(l, j):
        held = gathered[l][j]
        group = cap // 2 if cap % 2 == 0 else cap
        lines = pl.ds(j * part, part)

        def source(s):
            if l < 2:
                return held[s]
            return jnp.concatenate([held[0, s], held[1, s]], axis=0)

        def step(i, carry):
            base = i * group
            values = [
                jnp.dot(
                    source(sources[l, 0, base + u]), block_v[l, base + u],
                    preferred_element_type=jnp.float32,
                )
                for u in range(group)
            ]
            for u in range(group):
                s = l * cap + base + u
                run[s, lines] = values[u] + run[table[l, base + u], lines]
            return carry

        lax.fori_loop(0, cap // group, step, 0)

    def x_stage(l, j, value):
        kept = sums[l].at[j]
        for d in x_order:
            to = lax.rem(x + d, nx)

            def place(m, carry):
                kept[d - 1, m] = value(to, m).astype(jnp.bfloat16)
                return carry

            lax.fori_loop(0, ny, place, 0)
            send(kept.at[d - 1], xa[l].at[j, d - 1], f"x{l + 1}", j, x_peer(d), xa[l].at[j])

    def y_stage(l, j, value):
        arrive(f"x{l + 1}", j)

        def add(m, carry):
            total = value(x, m)
            for d in range(nx - 1):
                total = total + xa[l][j, d, m].astype(jnp.float32)
            y_in[l][j, m] = total.astype(jnp.bfloat16)
            return carry

        lax.fori_loop(0, ny, add, 0)
        for d in y_order:
            to = lax.rem(y + d, ny)
            send(y_in[l].at[j, to], ya[l].at[j, d - 1], f"y{l + 1}", j, y_peer(d), ya[l].at[j])

    def incoming(l, j):
        arrive(f"y{l + 1}", j)
        total = y_in[l][j, y].astype(jnp.float32)
        for d in range(ny - 1):
            total = total + ya[l][j, d].astype(jnp.float32)
        return total

    def own_value(l, lines):
        return lambda to, m: run[table[3 + l, m * nx + to], lines]

    def sub_lines(j):
        return pl.ds(j * part, part)

    def top_lines(j, h):
        return pl.ds(pl.multiple_of(j * part + h * fine, fine), fine)

    def merged(l, j):
        def value(to, m):
            own = run[table[3 + l, m * nx + to], top_lines(j, k)]
            return own + take[l - 1, j, m, to].astype(jnp.float32)

        return value

    def core_stage(l, j):
        kept = give.at[l - 1, j]

        def place(m, carry):
            for to in range(nx):
                kept[m, to] = run[table[3 + l, m * nx + to], top_lines(j, 1 - k)].astype(jnp.bfloat16)
            return carry

        lax.fori_loop(0, ny, place, 0)
        send(kept, take.at[l - 1, j], f"c{l + 1}", j, core, take.at[l - 1, j])

    def top_solve(l, j):
        lines = pl.ds(pl.multiple_of(k * part + j * fine, fine), fine)
        return solve(l + 1, given_t[l + 1, lines] - incoming(l, j))

    def emit(out, n, pieces):
        whole = jnp.concatenate(
            [pieces(j, h) for h in range(2) for j in range(PARTS)], axis=0
        )
        out[n] = whole.astype(jnp.float32).T.astype(jnp.bfloat16)

    to_scalars.wait()
    turn(0)
    pl.semaphore_wait(barrier, len(partners))

    parts = range(PARTS)
    for j in parts:
        share(0, j, solve(0, of_part(0, j)))
    for j in parts:
        arrive("g0", j)
        products(0, j)
        x_stage(0, j, own_value(0, sub_lines(j)))
    turn(1)
    for j in parts:
        y_stage(0, j, own_value(0, sub_lines(j)))
    for j in parts:
        share(1, j, solve(1, of_part(1, j) - incoming(0, j)))
    for j in parts:
        arrive("g1", j)
        products(1, j)
        core_stage(1, j)
    for j in parts:
        arrive("c2", j)
        x_stage(1, j, merged(1, j))
    turn(2)
    for j in parts:
        y_stage(1, j, merged(1, j))
    for j in parts:
        held = gathered[2][j]
        solved = top_solve(1, j)
        held[k, c] = solved
        for d in z_order:
            send(held.at[k, c], held.at[k, c], "g2", j, z_peer(d), held.at[0, pl.ds(0, nc - 1)])
    for j in parts:
        held = gathered[2][j]
        arrive("g2", j)
        send(held.at[k], held.at[k], "f2", j, core, held.at[0])
    for n in range(2):
        emit(out_sub, n, lambda j, h, n=n: gathered[n][j][c, pl.ds(h * fine, fine)])
    for j in parts:
        arrive("f2", j)
        products(2, j)
        core_stage(2, j)
    for j in parts:
        arrive("c3", j)
        x_stage(2, j, merged(2, j))
    for j in parts:
        y_stage(2, j, merged(2, j))
    emit(out_top, 0, lambda j, h: gathered[2][j][h, c])
    for j in parts:
        solved = top_solve(2, j)
        top[j, k] = solved
        send(top.at[j, k], top.at[j, k], "f3", j, core, top.at[j, 0])
    for j in parts:
        arrive("f3", j)
    emit(out_top, 1, lambda j, h: top[j, h])
    finish()


def local(nx, axis_sizes, blocks, sources, targets, counts, given_sub, given_top, inverse_sub, inverse_top):
    rows, nc = axis_sizes
    ny = rows // nx
    levels, cap, width = blocks.shape[3:6]
    sides = given_sub.shape[-1]
    part = sides // PARTS
    fine = part // 2
    sizes = (nx, ny, nc, cap, width, sides)
    bf16 = jnp.bfloat16

    def exchange(height):
        return [
            pltpu.VMEM((PARTS, nx - 1, ny, height, width), bf16),
            pltpu.VMEM((PARTS, nx - 1, ny, height, width), bf16),
            pltpu.VMEM((PARTS, ny, height, width), bf16),
            pltpu.VMEM((PARTS, ny - 1, height, width), bf16),
        ]

    smem = pl.BlockSpec(memory_space=pltpu.SMEM)
    anywhere = pl.BlockSpec(memory_space=pltpu.HBM)
    vmem = pl.BlockSpec(memory_space=pltpu.VMEM)
    semaphores = len(STEPS) * PARTS
    solved_sub, solved_top = pl.pallas_call(
        functools.partial(kernel, sizes),
        out_shape=(
            jax.ShapeDtypeStruct((2, width, sides), bf16),
            jax.ShapeDtypeStruct((2, width, sides), bf16),
        ),
        in_specs=[smem, smem, vmem] + [anywhere] * 5,
        out_specs=(vmem, vmem),
        scratch_shapes=[
            pltpu.VMEM((8, LANES), jnp.int32),
            pltpu.VMEM((8, LANES), jnp.int32),
            pltpu.SMEM((8, LANES), jnp.int32),
            pltpu.VMEM((levels, cap, width, width), bf16),
            pltpu.VMEM((4, width, sides), bf16),
            pltpu.VMEM((4, sides, width), jnp.float32),
            pltpu.VMEM((4, width, width), bf16),
            pltpu.VMEM((levels * cap + 1, sides, width), jnp.float32),
            pltpu.VMEM((PARTS, 2, fine, width), bf16),
            *[pltpu.VMEM((nc, part, width), bf16)] * (2 * PARTS),
            *[pltpu.VMEM((2, nc, fine, width), bf16)] * PARTS,
            *exchange(part),
            *exchange(fine),
            *exchange(fine),
            pltpu.VMEM((2, PARTS, ny, nx, fine, width), bf16),
            pltpu.VMEM((2, PARTS, ny, nx, fine, width), bf16),
            pltpu.SemaphoreType.DMA,
            pltpu.SemaphoreType.DMA((3,)),
            pltpu.SemaphoreType.DMA((8,)),
            pltpu.SemaphoreType.DMA((semaphores,)),
            pltpu.SemaphoreType.DMA((semaphores,)),
        ],
        compiler_params=pltpu.CompilerParams(
            collective_id=0, has_side_effects=True, vmem_limit_bytes=60 * 1024 * 1024
        ),
        name="substitution",
    )(
        sources.reshape(levels, 1, cap), counts.reshape(1, levels), targets.reshape(levels, 1, cap), blocks[0, 0, 0], given_sub[0, 0, 0], given_top[0, 0],
        inverse_sub[0, 0, 0], inverse_top[0, 0],
    )
    return solved_sub[None, None, None], solved_top[None, None]


def solution(mesh):
    nx = X_CHIPS
    in_specs = (
        P("prow", "pcol", "zgrid", None, None, None, None),
        P("prow", "pcol", "zgrid", None, None),
        P("prow", "pcol", "zgrid", None, None),
        P("prow", "pcol", "zgrid", None),
        P("prow", "pcol", "zgrid", None, None, None),
        P("prow", "pcol", None, None, None),
        P("prow", "pcol", "zgrid", None, None, None),
        P("prow", "pcol", None, None, None),
    )
    out_specs = (P("prow", "pcol", "zgrid", None, None, None), P("prow", "pcol", None, None, None))
    body = functools.partial(local, nx, (mesh.shape["prow"], mesh.shape["pcol"]))
    return jax.shard_map(body, mesh=mesh, in_specs=in_specs, out_specs=out_specs, check_vma=False)
```

```python
import functools

import jax
import jax.numpy as jnp
from jax import lax
from jax.experimental import pallas as pl
from jax.experimental.pallas import tpu as pltpu
from jax.sharding import PartitionSpec as P

MESH = pl.DeviceIdType.MESH
X_CHIPS = 4
PARTS = 2
LANES = 128
STEPS = (
    "g0", "x1", "v1", "y1", "w1", "g1", "c2", "x2", "v2", "y2", "w2", "g2", "f2",
    "c3", "x3", "v3", "y3", "w3", "f3",
)


def drain(ref, sem):
    pltpu.make_async_copy(ref, ref, sem).wait()


def times_transposed(left, right):
    return lax.dot_general(
        left, right, (((1,), (1,)), ((), ())), preferred_element_type=jnp.float32
    )


def kernel(
    sizes, sources_h, counts_h, targets_h, blocks, given_sub, given_top, inverse_sub, inverse_top,
    out_sub, out_top, sources, counts, targets, index_sem, result, key_v, table_v, table, block_v, given_v, given_t, inverse_v, run, top, *rest
):
    nx, ny, nc, cap, width, sides = sizes
    rows = nx * ny
    slots = 3 * cap
    part = sides // PARTS
    fine = part // 2
    gathered = [rest[PARTS * l : PARTS * (l + 1)] for l in range(3)]
    rest = rest[3 * PARTS :]
    near_out, near_in, far_out, far_in, y_out, y_in, w_out, w_in = [
        [rest[8 * l + i] for l in range(3)] for i in range(8)
    ]
    give, take, table_sem, out_sem, load_sem, small_sem, send_sem, recv_sem = rest[24:]
    p = lax.axis_index("prow")
    c = lax.axis_index("pcol")
    k = lax.axis_index("zgrid")
    x = lax.rem(p, nx)
    y = lax.div(p, nx)

    def x_peer(d):
        return {"prow": y * nx + lax.rem(x + d, nx)}

    def y_peer(d):
        return {"prow": lax.rem(y + d, ny) * nx + x}

    def z_peer(d):
        return {"pcol": lax.rem(c + d, nc)}

    core = {"zgrid": 1 - k}
    near = [d for d in range(1, nx) if min(d, nx - d) == 1]
    far = [d for d in range(1, nx) if min(d, nx - d) > 1]
    y_order = sorted(range(1, ny), key=lambda d: -min(d, ny - d))
    z_order = sorted(range(1, nc), key=lambda d: -min(d, nc - d))
    pending = {}

    def sem_of(step, j):
        return STEPS.index(step) * PARTS + j

    def send(src, dst, step, j, device, everything):
        slot = sem_of(step, j)
        pending[slot] = everything
        pltpu.make_async_remote_copy(
            src_ref=src, dst_ref=dst, send_sem=send_sem.at[slot], recv_sem=recv_sem.at[slot],
            device_id=device, device_id_type=MESH,
        ).start()

    def arrive(step, j):
        slot = sem_of(step, j)
        drain(pending[slot], recv_sem.at[slot])

    def finish():
        for slot, everything in pending.items():
            drain(everything, send_sem.at[slot])

    loads = [pltpu.make_async_copy(blocks.at[l], block_v.at[l], load_sem.at[l]) for l in range(3)]
    smalls = []
    for n in range(4):
        g = given_sub.at[n] if n < 2 else given_top.at[n - 2]
        i = inverse_sub.at[n] if n < 2 else inverse_top.at[n - 2]
        smalls.append(pltpu.make_async_copy(g, given_v.at[n], small_sem.at[2 * n]))
        smalls.append(pltpu.make_async_copy(i, inverse_v.at[n], small_sem.at[2 * n + 1]))
    indices = [
        pltpu.make_async_copy(a, b, index_sem.at[n])
        for n, (a, b) in enumerate(((sources_h, sources), (counts_h, counts), (targets_h, targets)))
    ]
    for s in smalls[:2] + indices + smalls[2:]:
        s.start()
    for s in loads:
        s.start()

    barrier = pltpu.get_barrier_semaphore()
    partners = (
        [x_peer(d) for d in near + far] + [y_peer(d) for d in y_order]
        + [z_peer(d) for d in z_order] + [core]
    )
    for device in partners:
        pl.semaphore_signal(barrier, inc=1, device_id=device, device_id_type=MESH)

    def natural(j, h):
        return pl.ds(h * part + j * fine, fine)

    def of_part(l, j):
        return jnp.concatenate([given_t[l, natural(j, h)] for h in range(2)], axis=0)

    def solve(l, residual):
        solved = times_transposed(residual.astype(jnp.bfloat16), inverse_v[l])
        return solved.astype(jnp.bfloat16)

    def share(l, j, solved):
        held = gathered[l][j]
        held[c] = solved
        for d in z_order:
            send(held.at[c], held.at[c], f"g{l}", j, z_peer(d), held.at[pl.ds(0, nc - 1)])

    def turn(l):
        loads[l].wait()

        def step(i, carry):
            for u in range(4):
                block_v[l, i * 4 + u] = block_v[l, i * 4 + u].T
            return carry

        lax.fori_loop(0, cap // 4, step, 0)

    def products(l, j):
        held = gathered[l][j]
        group = cap // 2 if cap % 2 == 0 else cap
        lines = pl.ds(j * part, part)

        def source(s):
            if l < 2:
                return held[s]
            return jnp.concatenate([held[0, s], held[1, s]], axis=0)

        def step(i, carry):
            base = i * group
            values = [
                jnp.dot(
                    source(sources[l, 0, base + u]), block_v[l, base + u],
                    preferred_element_type=jnp.float32,
                )
                for u in range(group)
            ]
            for u in range(group):
                s = l * cap + base + u
                run[s, lines] = values[u] + run[table[l, base + u], lines]
            return carry

        lax.fori_loop(0, cap // group, step, 0)

    def first_stage(l, j, value):
        n = l + 1
        for f, d in enumerate(far):
            to = lax.rem(x + d, nx)

            def place_far(m, carry):
                far_out[l][j, f, m] = value(to, m).astype(jnp.bfloat16)
                return carry

            lax.fori_loop(0, ny, place_far, 0)
            for e in y_order:
                send(
                    far_out[l].at[j, f, lax.rem(y + e, ny)], far_in[l].at[j, f, e - 1],
                    f"v{n}", j, y_peer(e), far_in[l].at[j],
                )
        for f, d in enumerate(near):
            to = lax.rem(x + d, nx)

            def place_near(m, carry):
                near_out[l][j, f, m] = value(to, m).astype(jnp.bfloat16)
                return carry

            lax.fori_loop(0, ny, place_near, 0)
            send(near_out[l].at[j, f], near_in[l].at[j, f], f"x{n}", j, x_peer(d), near_in[l].at[j])

    def second_stage(l, j, value):
        n = l + 1
        arrive(f"x{n}", j)

        def add(m, carry):
            total = value(x, m)
            for f in range(len(near)):
                total = total + near_in[l][j, f, m].astype(jnp.float32)
            y_out[l][j, m] = total.astype(jnp.bfloat16)
            return carry

        lax.fori_loop(0, ny, add, 0)
        for e in y_order:
            send(y_out[l].at[j, lax.rem(y + e, ny)], y_in[l].at[j, e - 1], f"y{n}", j, y_peer(e), y_in[l].at[j])
        if far:
            arrive(f"v{n}", j)
        for f, d in enumerate(far):
            total = value(lax.rem(x + d, nx), y)
            for e in range(ny - 1):
                total = total + far_in[l][j, f, e].astype(jnp.float32)
            w_out[l][j, f] = total.astype(jnp.bfloat16)
            send(w_out[l].at[j, f], w_in[l].at[j, f], f"w{n}", j, x_peer(d), w_in[l].at[j])

    def incoming(l, j):
        n = l + 1
        arrive(f"y{n}", j)
        total = y_out[l][j, y].astype(jnp.float32)
        for e in range(ny - 1):
            total = total + y_in[l][j, e].astype(jnp.float32)
        if far:
            arrive(f"w{n}", j)
        for f in range(len(far)):
            total = total + w_in[l][j, f].astype(jnp.float32)
        return total

    def own_value(l, lines):
        return lambda to, m: run[table[3 + l, m * nx + to], lines]

    def sub_lines(j):
        return pl.ds(j * part, part)

    def top_lines(j, h):
        return pl.ds(pl.multiple_of(j * part + h * fine, fine), fine)

    def merged(l, j):
        def value(to, m):
            own = run[table[3 + l, m * nx + to], top_lines(j, k)]
            return own + take[l - 1, j, m, to].astype(jnp.float32)

        return value

    def core_stage(l, j):
        kept = give.at[l - 1, j]

        def place(m, carry):
            for to in range(nx):
                kept[m, to] = run[table[3 + l, m * nx + to], top_lines(j, 1 - k)].astype(jnp.bfloat16)
            return carry

        lax.fori_loop(0, ny, place, 0)
        send(kept, take.at[l - 1, j], f"c{l + 1}", j, core, take.at[l - 1, j])

    def top_solve(l, j):
        lines = pl.ds(pl.multiple_of(k * part + j * fine, fine), fine)
        return solve(l + 1, given_t[l + 1, lines] - incoming(l, j))

    def prepare():
        for s in indices:
            s.wait()
        lanes = lax.broadcasted_iota(jnp.int32, (1, LANES), 1)
        key_v[...] = jnp.full(key_v.shape, -1, jnp.int32)
        for l in range(3):
            live = lanes[:, :cap] < counts[0, l]
            key_v[l : l + 1, :cap] = jnp.where(live, targets[l], -1)
        key_rows = key_v[...]
        key_columns = key_rows.T
        line = lax.broadcasted_iota(jnp.int32, (LANES, LANES), 0)
        lane = lax.broadcasted_iota(jnp.int32, (LANES, LANES), 1)

        def latest(wanted, l, strict):
            best = jnp.full((1, LANES), -1, jnp.int32)
            for m in range(l + 1):
                hit = (key_columns[:, m : m + 1] == wanted) & (wanted >= 0)
                if m == l and strict:
                    hit = hit & (line < lane)
                best = jnp.maximum(best, jnp.max(jnp.where(hit, line + m * cap, -1), axis=0, keepdims=True))
            return jnp.where(best < 0, slots, best)

        for l in range(3):
            table_v[l : l + 1] = latest(key_rows[l : l + 1], l, True)
            table_v[3 + l : 4 + l] = latest(lanes + l * rows, l, False)
        to_scalars = pltpu.make_async_copy(table_v, table, table_sem)
        to_scalars.start()
        run[slots] = jnp.zeros((sides, width), jnp.float32)
        for l in range(1, 4):
            smalls[2 * l].wait()
            smalls[2 * l + 1].wait()
            given_t[l] = given_v[l].astype(jnp.float32).T
        turn(0)
        to_scalars.wait()

    writes = []

    def emit(n, pieces):
        whole = jnp.concatenate(
            [pieces(j, h) for h in range(2) for j in range(PARTS)], axis=0
        )
        result[n] = whole.astype(jnp.float32).T.astype(jnp.bfloat16)
        out = out_sub.at[n] if n < 2 else out_top.at[n - 2]
        writes.append(pltpu.make_async_copy(result.at[n], out, out_sem.at[n]))
        writes[-1].start()

    smalls[0].wait()
    smalls[1].wait()
    given_t[0] = given_v[0].astype(jnp.float32).T
    parts = range(PARTS)
    firsts = [solve(0, of_part(0, j)) for j in parts]
    pl.semaphore_wait(barrier, len(partners))
    for j in parts:
        share(0, j, firsts[j])
    prepare()
    for j in parts:
        arrive("g0", j)
        products(0, j)
        first_stage(0, j, own_value(0, sub_lines(j)))
    turn(1)
    for j in parts:
        second_stage(0, j, own_value(0, sub_lines(j)))
    for j in parts:
        share(1, j, solve(1, of_part(1, j) - incoming(0, j)))
    for j in parts:
        arrive("g1", j)
        products(1, j)
        core_stage(1, j)
    for j in parts:
        arrive("c2", j)
        first_stage(1, j, merged(1, j))
    turn(2)
    for j in parts:
        second_stage(1, j, merged(1, j))
    for j in parts:
        held = gathered[2][j]
        solved = top_solve(1, j)
        held[k, c] = solved
        for d in z_order:
            send(held.at[k, c], held.at[k, c], "g2", j, z_peer(d), held.at[0, pl.ds(0, nc - 1)])
    for j in parts:
        held = gathered[2][j]
        arrive("g2", j)
        send(held.at[k], held.at[k], "f2", j, core, held.at[0])
    for n in range(2):
        emit(n, lambda j, h, n=n: gathered[n][j][c, pl.ds(h * fine, fine)])
    for j in parts:
        arrive("f2", j)
        products(2, j)
        core_stage(2, j)
    for j in parts:
        arrive("c3", j)
        first_stage(2, j, merged(2, j))
    for j in parts:
        second_stage(2, j, merged(2, j))
    emit(2, lambda j, h: gathered[2][j][h, c])
    for j in parts:
        solved = top_solve(2, j)
        top[j, k] = solved
        send(top.at[j, k], top.at[j, k], "f3", j, core, top.at[j, 0])
    for j in parts:
        arrive("f3", j)
    emit(3, lambda j, h: top[j, h])
    for w in writes:
        w.wait()
    finish()


def copy_kernel(sub, top, out_sub, out_top, sub_v, top_v, sems):
    reads = (
        pltpu.make_async_copy(sub, sub_v, sems.at[0]),
        pltpu.make_async_copy(top, top_v, sems.at[1]),
    )
    writes = (
        pltpu.make_async_copy(sub_v, out_sub, sems.at[2]),
        pltpu.make_async_copy(top_v, out_top, sems.at[3]),
    )
    for r in reads:
        r.start()
    for r, w in zip(reads, writes):
        r.wait()
        w.start()
    for w in writes:
        w.wait()


def local(nx, axis_sizes, blocks, sources, targets, counts, given_sub, given_top, inverse_sub, inverse_top):
    rows, nc = axis_sizes
    ny = rows // nx
    levels, cap, width = blocks.shape[3:6]
    sides = given_sub.shape[-1]
    part = sides // PARTS
    fine = part // 2
    sizes = (nx, ny, nc, cap, width, sides)
    bf16 = jnp.bfloat16

    near = min(2, nx - 1)
    far = nx - 1 - near

    def exchange(height):
        block = (height, width)
        return [
            pltpu.VMEM((PARTS, near, ny) + block, bf16),
            pltpu.VMEM((PARTS, near, ny) + block, bf16),
            pltpu.VMEM((PARTS, max(far, 1), ny) + block, bf16),
            pltpu.VMEM((PARTS, max(far, 1), ny - 1) + block, bf16),
            pltpu.VMEM((PARTS, ny) + block, bf16),
            pltpu.VMEM((PARTS, ny - 1) + block, bf16),
            pltpu.VMEM((PARTS, max(far, 1)) + block, bf16),
            pltpu.VMEM((PARTS, max(far, 1)) + block, bf16),
        ]

    anywhere = pl.BlockSpec(memory_space=pltpu.HBM)
    semaphores = len(STEPS) * PARTS
    solved_sub, solved_top = pl.pallas_call(
        functools.partial(kernel, sizes),
        out_shape=(
            jax.ShapeDtypeStruct((2, width, sides), bf16),
            jax.ShapeDtypeStruct((2, width, sides), bf16),
        ),
        in_specs=[anywhere] * 8,
        out_specs=(anywhere, anywhere),
        scratch_shapes=[
            pltpu.SMEM((levels, 1, cap), jnp.int32),
            pltpu.SMEM((1, levels), jnp.int32),
            pltpu.VMEM((levels, 1, cap), jnp.int32),
            pltpu.SemaphoreType.DMA((3,)),
            pltpu.VMEM((4, width, sides), bf16),
            pltpu.VMEM((8, LANES), jnp.int32),
            pltpu.VMEM((8, LANES), jnp.int32),
            pltpu.SMEM((8, LANES), jnp.int32),
            pltpu.VMEM((levels, cap, width, width), bf16),
            pltpu.VMEM((4, width, sides), bf16),
            pltpu.VMEM((4, sides, width), jnp.float32),
            pltpu.VMEM((4, width, width), bf16),
            pltpu.VMEM((levels * cap + 1, sides, width), jnp.float32),
            pltpu.VMEM((PARTS, 2, fine, width), bf16),
            *[pltpu.VMEM((nc, part, width), bf16)] * (2 * PARTS),
            *[pltpu.VMEM((2, nc, fine, width), bf16)] * PARTS,
            *exchange(part),
            *exchange(fine),
            *exchange(fine),
            pltpu.VMEM((2, PARTS, ny, nx, fine, width), bf16),
            pltpu.VMEM((2, PARTS, ny, nx, fine, width), bf16),
            pltpu.SemaphoreType.DMA,
            pltpu.SemaphoreType.DMA((4,)),
            pltpu.SemaphoreType.DMA((3,)),
            pltpu.SemaphoreType.DMA((8,)),
            pltpu.SemaphoreType.DMA((semaphores,)),
            pltpu.SemaphoreType.DMA((semaphores,)),
        ],
        compiler_params=pltpu.CompilerParams(
            collective_id=0, has_side_effects=True, vmem_limit_bytes=60 * 1024 * 1024
        ),
        name="substitution",
    )(
        sources.reshape(levels, 1, cap), counts.reshape(1, levels), targets.reshape(levels, 1, cap), blocks[0, 0, 0], given_sub[0, 0, 0], given_top[0, 0],
        inverse_sub[0, 0, 0], inverse_top[0, 0],
    )
    solved_sub, solved_top = pl.pallas_call(
        copy_kernel,
        out_shape=(
            jax.ShapeDtypeStruct((2, width, sides), bf16),
            jax.ShapeDtypeStruct((2, width, sides), bf16),
        ),
        in_specs=[anywhere] * 2,
        out_specs=(anywhere, anywhere),
        scratch_shapes=[
            pltpu.VMEM((2, width, sides), bf16),
            pltpu.VMEM((2, width, sides), bf16),
            pltpu.SemaphoreType.DMA((4,)),
        ],
        compiler_params=pltpu.CompilerParams(vmem_limit_bytes=60 * 1024 * 1024),
        name="hand_over",
    )(solved_sub, solved_top)
    return solved_sub[None, None, None], solved_top[None, None]


def solution(mesh):
    nx = X_CHIPS
    in_specs = (
        P("prow", "pcol", "zgrid", None, None, None, None),
        P("prow", "pcol", "zgrid", None, None),
        P("prow", "pcol", "zgrid", None, None),
        P("prow", "pcol", "zgrid", None),
        P("prow", "pcol", "zgrid", None, None, None),
        P("prow", "pcol", None, None, None),
        P("prow", "pcol", "zgrid", None, None, None),
        P("prow", "pcol", None, None, None),
    )
    out_specs = (P("prow", "pcol", "zgrid", None, None, None), P("prow", "pcol", None, None, None))
    body = functools.partial(local, nx, (mesh.shape["prow"], mesh.shape["pcol"]))
    return jax.shard_map(body, mesh=mesh, in_specs=in_specs, out_specs=out_specs, check_vma=False)
```

```python
import functools

import jax
import jax.numpy as jnp
from jax import lax
from jax.experimental import pallas as pl
from jax.experimental.pallas import tpu as pltpu
from jax.sharding import PartitionSpec as P

MESH = pl.DeviceIdType.MESH
X_CHIPS = 4
PARTS = 4
LANES = 128
STEPS = (
    "g0", "x1", "v1", "y1", "w1", "g1", "x2", "v2", "y2", "w2", "g2", "f2",
    "x3", "v3", "y3", "w3", "f3",
)


def drain(ref, sem):
    pltpu.make_async_copy(ref, ref, sem).wait()


def times_transposed(left, right):
    return lax.dot_general(
        left, right, (((1,), (1,)), ((), ())), preferred_element_type=jnp.float32
    )


def kernel(
    sizes, sources_h, counts_h, targets_h, blocks, given_sub, given_top, inverse_sub, inverse_top,
    out_sub, out_top, sources, counts, targets, index_sem, result, key_v, table_v, table, block_v, given_v, given_t, inverse_v, run, top, *rest
):
    nx, ny, nc, cap, width, sides = sizes
    rows = nx * ny
    slots = 3 * cap
    part = sides // PARTS
    fine = part // 2
    gathered = [rest[PARTS * l : PARTS * (l + 1)] for l in range(3)]
    rest = rest[3 * PARTS :]
    near_out, near_in, far_out, far_in, y_out, y_in, w_out, w_in = [
        [rest[8 * l + i] for l in range(3)] for i in range(8)
    ]
    own_out, table_sem, out_sem, load_sem, small_sem, send_sem, recv_sem = rest[24:]
    p = lax.axis_index("prow")
    c = lax.axis_index("pcol")
    k = lax.axis_index("zgrid")
    x = lax.rem(p, nx)
    y = lax.div(p, nx)

    def x_peer(d):
        return {"prow": y * nx + lax.rem(x + d, nx)}

    def y_peer(d):
        return {"prow": lax.rem(y + d, ny) * nx + x}

    def z_peer(d):
        return {"pcol": lax.rem(c + d, nc)}

    core = {"zgrid": 1 - k}

    def across(device):
        return dict(device, zgrid=1 - k)

    def on_core(device, h):
        return dict(device, zgrid=h)

    near = [d for d in range(1, nx) if min(d, nx - d) == 1]
    far = [d for d in range(1, nx) if min(d, nx - d) > 1]
    y_order = sorted(range(1, ny), key=lambda d: -min(d, ny - d))
    z_order = sorted(range(1, nc), key=lambda d: -min(d, nc - d))
    pending = {}

    def sem_of(step, j):
        return STEPS.index(step) * PARTS + j

    def send(src, dst, step, j, device, everything):
        slot = sem_of(step, j)
        pending[slot] = everything
        pltpu.make_async_remote_copy(
            src_ref=src, dst_ref=dst, send_sem=send_sem.at[slot], recv_sem=recv_sem.at[slot],
            device_id=device, device_id_type=MESH,
        ).start()

    def arrive(step, j):
        slot = sem_of(step, j)
        drain(pending[slot], recv_sem.at[slot])

    def finish():
        for slot, everything in pending.items():
            drain(everything, send_sem.at[slot])

    loads = [pltpu.make_async_copy(blocks.at[l], block_v.at[l], load_sem.at[l]) for l in range(3)]
    smalls = []
    for n in range(4):
        g = given_sub.at[n] if n < 2 else given_top.at[n - 2]
        i = inverse_sub.at[n] if n < 2 else inverse_top.at[n - 2]
        smalls.append(pltpu.make_async_copy(g, given_v.at[n], small_sem.at[2 * n]))
        smalls.append(pltpu.make_async_copy(i, inverse_v.at[n], small_sem.at[2 * n + 1]))
    indices = [
        pltpu.make_async_copy(a, b, index_sem.at[n])
        for n, (a, b) in enumerate(((sources_h, sources), (counts_h, counts), (targets_h, targets)))
    ]
    for s in smalls[:2] + indices + smalls[2:]:
        s.start()
    for s in loads:
        s.start()

    barrier = pltpu.get_barrier_semaphore()
    partners = (
        [x_peer(d) for d in near + far] + [across(x_peer(d)) for d in near]
        + [y_peer(d) for d in y_order] + [across(y_peer(d)) for d in (y_order if far else [])]
        + [z_peer(d) for d in z_order] + [core]
    )
    for device in partners:
        pl.semaphore_signal(barrier, inc=1, device_id=device, device_id_type=MESH)

    def natural(j, h):
        return pl.ds(h * (sides // 2) + j * fine, fine)

    def of_part(l, j):
        return jnp.concatenate([given_t[l, natural(j, h)] for h in range(2)], axis=0)

    def solve(l, residual):
        solved = times_transposed(residual.astype(jnp.bfloat16), inverse_v[l])
        return solved.astype(jnp.bfloat16)

    def share(l, j, solved):
        held = gathered[l][j]
        held[c] = solved
        for d in z_order:
            send(held.at[c], held.at[c], f"g{l}", j, z_peer(d), held.at[pl.ds(0, nc - 1)])

    def turn(l):
        loads[l].wait()

        def step(i, carry):
            for u in range(4):
                block_v[l, i * 4 + u] = block_v[l, i * 4 + u].T
            return carry

        lax.fori_loop(0, cap // 4, step, 0)

    def products(l, j):
        held = gathered[l][j]
        group = cap // 2 if cap % 2 == 0 else cap
        lines = pl.ds(j * part, part)

        def source(s):
            if l < 2:
                return held[s]
            return jnp.concatenate([held[0, s], held[1, s]], axis=0)

        def step(i, carry):
            base = i * group
            values = [
                jnp.dot(
                    source(sources[l, 0, base + u]), block_v[l, base + u],
                    preferred_element_type=jnp.float32,
                )
                for u in range(group)
            ]
            for u in range(group):
                s = l * cap + base + u
                run[s, lines] = values[u] + run[table[l, base + u], lines]
            return carry

        lax.fori_loop(0, cap // group, step, 0)

    def first_stage(l, j, value):
        n = l + 1
        for f, d in enumerate(far):
            to = lax.rem(x + d, nx)

            def place_far(m, carry):
                far_out[l][j, f, m] = value(to, m).astype(jnp.bfloat16)
                return carry

            lax.fori_loop(0, ny, place_far, 0)
            for e in y_order:
                send(
                    far_out[l].at[j, f, lax.rem(y + e, ny)], far_in[l].at[j, f, e - 1],
                    f"v{n}", j, y_peer(e), far_in[l].at[j],
                )
        for f, d in enumerate(near):
            to = lax.rem(x + d, nx)

            def place_near(m, carry):
                near_out[l][j, f, m] = value(to, m).astype(jnp.bfloat16)
                return carry

            lax.fori_loop(0, ny, place_near, 0)
            send(near_out[l].at[j, f], near_in[l].at[j, f], f"x{n}", j, x_peer(d), near_in[l].at[j])

    def first_stage_top(l, j):
        n = l + 1
        lines = sub_lines(j)

        def split(kept, to):
            def place(m, carry):
                block = run[table[3 + l, m * nx + to], lines].astype(jnp.bfloat16)
                kept[0, m] = block[:fine]
                kept[1, m] = block[fine:]
                return carry

            lax.fori_loop(0, ny, place, 0)

        for f, d in enumerate(far):
            kept = far_out[l].at[j, f]
            split(kept, lax.rem(x + d, nx))
            for e in y_order:
                for h in range(2):
                    send(
                        kept.at[h, lax.rem(y + e, ny)], far_in[l].at[j, f, k * (ny - 1) + e - 1],
                        f"v{n}", j, on_core(y_peer(e), h), far_in[l].at[j],
                    )
            send(kept.at[1 - k, y], far_in[l].at[j, f, 2 * (ny - 1)], f"v{n}", j, core, far_in[l].at[j])
        for f, d in enumerate(near):
            kept = near_out[l].at[j, f]
            split(kept, lax.rem(x + d, nx))
            for h in range(2):
                send(
                    kept.at[h], near_in[l].at[j, 2 * f + k], f"x{n}", j,
                    on_core(x_peer(d), h), near_in[l].at[j],
                )

        def place_own(m, carry):
            own_out[l - 1, j, m] = run[table[3 + l, m * nx + x], top_lines(j, 1 - k)].astype(jnp.bfloat16)
            return carry

        lax.fori_loop(0, ny, place_own, 0)
        send(own_out.at[l - 1, j], near_in[l].at[j, 2 * len(near)], f"x{n}", j, core, near_in[l].at[j])

    def second_stage(l, j, value):
        n = l + 1
        arrive(f"x{n}", j)
        near_count = len(near) if l == 0 else 2 * len(near) + 1
        far_count = ny - 1 if l == 0 else 2 * (ny - 1) + 1

        def add(m, carry):
            total = value(x, m)
            for f in range(near_count):
                total = total + near_in[l][j, f, m].astype(jnp.float32)
            y_out[l][j, m] = total.astype(jnp.bfloat16)
            return carry

        lax.fori_loop(0, ny, add, 0)
        for e in y_order:
            send(y_out[l].at[j, lax.rem(y + e, ny)], y_in[l].at[j, e - 1], f"y{n}", j, y_peer(e), y_in[l].at[j])
        if far:
            arrive(f"v{n}", j)
        for f, d in enumerate(far):
            total = value(lax.rem(x + d, nx), y)
            for e in range(far_count):
                total = total + far_in[l][j, f, e].astype(jnp.float32)
            w_out[l][j, f] = total.astype(jnp.bfloat16)
            send(w_out[l].at[j, f], w_in[l].at[j, f], f"w{n}", j, x_peer(d), w_in[l].at[j])

    def incoming(l, j):
        n = l + 1
        arrive(f"y{n}", j)
        total = y_out[l][j, y].astype(jnp.float32)
        for e in range(ny - 1):
            total = total + y_in[l][j, e].astype(jnp.float32)
        if far:
            arrive(f"w{n}", j)
        for f in range(len(far)):
            total = total + w_in[l][j, f].astype(jnp.float32)
        return total

    def own_value(l, lines):
        return lambda to, m: run[table[3 + l, m * nx + to], lines]

    def sub_lines(j):
        return pl.ds(j * part, part)

    def top_lines(j, h):
        return pl.ds(pl.multiple_of(j * part + h * fine, fine), fine)

    def top_solve(l, j):
        lines = pl.ds(pl.multiple_of(k * (sides // 2) + j * fine, fine), fine)
        return solve(l + 1, given_t[l + 1, lines] - incoming(l, j))

    def prepare():
        for s in indices:
            s.wait()
        lanes = lax.broadcasted_iota(jnp.int32, (1, LANES), 1)
        key_v[...] = jnp.full(key_v.shape, -1, jnp.int32)
        for l in range(3):
            live = lanes[:, :cap] < counts[0, l]
            key_v[l : l + 1, :cap] = jnp.where(live, targets[l], -1)
        key_rows = key_v[...]
        key_columns = key_rows.T
        line = lax.broadcasted_iota(jnp.int32, (LANES, LANES), 0)
        lane = lax.broadcasted_iota(jnp.int32, (LANES, LANES), 1)

        def latest(wanted, l, strict):
            best = jnp.full((1, LANES), -1, jnp.int32)
            for m in range(l + 1):
                hit = (key_columns[:, m : m + 1] == wanted) & (wanted >= 0)
                if m == l and strict:
                    hit = hit & (line < lane)
                best = jnp.maximum(best, jnp.max(jnp.where(hit, line + m * cap, -1), axis=0, keepdims=True))
            return jnp.where(best < 0, slots, best)

        for l in range(3):
            table_v[l : l + 1] = latest(key_rows[l : l + 1], l, True)
            table_v[3 + l : 4 + l] = latest(lanes + l * rows, l, False)
        to_scalars = pltpu.make_async_copy(table_v, table, table_sem)
        to_scalars.start()
        run[slots] = jnp.zeros((sides, width), jnp.float32)
        for l in range(1, 4):
            smalls[2 * l].wait()
            smalls[2 * l + 1].wait()
            given_t[l] = given_v[l].astype(jnp.float32).T
        turn(0)
        to_scalars.wait()

    writes = []

    def emit(n, pieces):
        whole = jnp.concatenate(
            [pieces(j, h) for h in range(2) for j in range(PARTS)], axis=0
        )
        result[n] = whole.astype(jnp.float32).T.astype(jnp.bfloat16)
        out = out_sub.at[n] if n < 2 else out_top.at[n - 2]
        writes.append(pltpu.make_async_copy(result.at[n], out, out_sem.at[n]))
        writes[-1].start()

    smalls[0].wait()
    smalls[1].wait()
    given_t[0] = given_v[0].astype(jnp.float32).T
    parts = range(PARTS)
    firsts = [solve(0, of_part(0, j)) for j in parts]
    pl.semaphore_wait(barrier, len(partners))
    for j in parts:
        share(0, j, firsts[j])
    prepare()
    for j in parts:
        arrive("g0", j)
        products(0, j)
        first_stage(0, j, own_value(0, sub_lines(j)))
    turn(1)
    for j in parts:
        second_stage(0, j, own_value(0, sub_lines(j)))
    for j in parts:
        share(1, j, solve(1, of_part(1, j) - incoming(0, j)))
    for j in parts:
        arrive("g1", j)
        products(1, j)
        first_stage_top(1, j)
    turn(2)
    for j in parts:
        second_stage(1, j, own_value(1, top_lines(j, k)))
    for j in parts:
        held = gathered[2][j]
        solved = top_solve(1, j)
        held[k, c] = solved
        for d in z_order:
            send(held.at[k, c], held.at[k, c], "g2", j, z_peer(d), held.at[0, pl.ds(0, nc - 1)])
    for j in parts:
        held = gathered[2][j]
        arrive("g2", j)
        send(held.at[k], held.at[k], "f2", j, core, held.at[0])
    for n in range(2):
        emit(n, lambda j, h, n=n: gathered[n][j][c, pl.ds(h * fine, fine)])
    for j in parts:
        arrive("f2", j)
        products(2, j)
        first_stage_top(2, j)
    for j in parts:
        second_stage(2, j, own_value(2, top_lines(j, k)))
    emit(2, lambda j, h: gathered[2][j][h, c])
    for j in parts:
        solved = top_solve(2, j)
        top[j, k] = solved
        send(top.at[j, k], top.at[j, k], "f3", j, core, top.at[j, 0])
    for j in parts:
        arrive("f3", j)
    emit(3, lambda j, h: top[j, h])
    for w in writes:
        w.wait()
    finish()


def copy_kernel(sub, top, out_sub, out_top, sub_v, top_v, sems):
    reads = (
        pltpu.make_async_copy(sub, sub_v, sems.at[0]),
        pltpu.make_async_copy(top, top_v, sems.at[1]),
    )
    writes = (
        pltpu.make_async_copy(sub_v, out_sub, sems.at[2]),
        pltpu.make_async_copy(top_v, out_top, sems.at[3]),
    )
    for r in reads:
        r.start()
    for r, w in zip(reads, writes):
        r.wait()
        w.start()
    for w in writes:
        w.wait()


def local(nx, axis_sizes, blocks, sources, targets, counts, given_sub, given_top, inverse_sub, inverse_top):
    rows, nc = axis_sizes
    ny = rows // nx
    levels, cap, width = blocks.shape[3:6]
    sides = given_sub.shape[-1]
    part = sides // PARTS
    fine = part // 2
    sizes = (nx, ny, nc, cap, width, sides)
    bf16 = jnp.bfloat16

    near = min(2, nx - 1)
    far = nx - 1 - near

    def exchange(height, split):
        block = (height, width)
        halves = (2,) if split else ()
        return [
            pltpu.VMEM((PARTS, near) + halves + (ny,) + block, bf16),
            pltpu.VMEM((PARTS, 2 * near + 1 if split else near, ny) + block, bf16),
            pltpu.VMEM((PARTS, max(far, 1)) + halves + (ny,) + block, bf16),
            pltpu.VMEM((PARTS, max(far, 1), 2 * ny - 1 if split else ny - 1) + block, bf16),
            pltpu.VMEM((PARTS, ny) + block, bf16),
            pltpu.VMEM((PARTS, ny - 1) + block, bf16),
            pltpu.VMEM((PARTS, max(far, 1)) + block, bf16),
            pltpu.VMEM((PARTS, max(far, 1)) + block, bf16),
        ]

    anywhere = pl.BlockSpec(memory_space=pltpu.HBM)
    semaphores = len(STEPS) * PARTS
    solved_sub, solved_top = pl.pallas_call(
        functools.partial(kernel, sizes),
        out_shape=(
            jax.ShapeDtypeStruct((2, width, sides), bf16),
            jax.ShapeDtypeStruct((2, width, sides), bf16),
        ),
        in_specs=[anywhere] * 8,
        out_specs=(anywhere, anywhere),
        scratch_shapes=[
            pltpu.SMEM((levels, 1, cap), jnp.int32),
            pltpu.SMEM((1, levels), jnp.int32),
            pltpu.VMEM((levels, 1, cap), jnp.int32),
            pltpu.SemaphoreType.DMA((3,)),
            pltpu.VMEM((4, width, sides), bf16),
            pltpu.VMEM((8, LANES), jnp.int32),
            pltpu.VMEM((8, LANES), jnp.int32),
            pltpu.SMEM((8, LANES), jnp.int32),
            pltpu.VMEM((levels, cap, width, width), bf16),
            pltpu.VMEM((4, width, sides), bf16),
            pltpu.VMEM((4, sides, width), jnp.float32),
            pltpu.VMEM((4, width, width), bf16),
            pltpu.VMEM((levels * cap + 1, sides, width), jnp.float32),
            pltpu.VMEM((PARTS, 2, fine, width), bf16),
            *[pltpu.VMEM((nc, part, width), bf16)] * (2 * PARTS),
            *[pltpu.VMEM((2, nc, fine, width), bf16)] * PARTS,
            *exchange(part, False),
            *exchange(fine, True),
            *exchange(fine, True),
            pltpu.VMEM((2, PARTS, ny, fine, width), bf16),
            pltpu.SemaphoreType.DMA,
            pltpu.SemaphoreType.DMA((4,)),
            pltpu.SemaphoreType.DMA((3,)),
            pltpu.SemaphoreType.DMA((8,)),
            pltpu.SemaphoreType.DMA((semaphores,)),
            pltpu.SemaphoreType.DMA((semaphores,)),
        ],
        compiler_params=pltpu.CompilerParams(
            collective_id=0, has_side_effects=True, vmem_limit_bytes=60 * 1024 * 1024
        ),
        name="substitution",
    )(
        sources.reshape(levels, 1, cap), counts.reshape(1, levels), targets.reshape(levels, 1, cap), blocks[0, 0, 0], given_sub[0, 0, 0], given_top[0, 0],
        inverse_sub[0, 0, 0], inverse_top[0, 0],
    )
    solved_sub, solved_top = pl.pallas_call(
        copy_kernel,
        out_shape=(
            jax.ShapeDtypeStruct((2, width, sides), bf16),
            jax.ShapeDtypeStruct((2, width, sides), bf16),
        ),
        in_specs=[anywhere] * 2,
        out_specs=(anywhere, anywhere),
        scratch_shapes=[
            pltpu.VMEM((2, width, sides), bf16),
            pltpu.VMEM((2, width, sides), bf16),
            pltpu.SemaphoreType.DMA((4,)),
        ],
        compiler_params=pltpu.CompilerParams(vmem_limit_bytes=60 * 1024 * 1024),
        name="hand_over",
    )(solved_sub, solved_top)
    return solved_sub[None, None, None], solved_top[None, None]


def solution(mesh):
    nx = X_CHIPS
    in_specs = (
        P("prow", "pcol", "zgrid", None, None, None, None),
        P("prow", "pcol", "zgrid", None, None),
        P("prow", "pcol", "zgrid", None, None),
        P("prow", "pcol", "zgrid", None),
        P("prow", "pcol", "zgrid", None, None, None),
        P("prow", "pcol", None, None, None),
        P("prow", "pcol", "zgrid", None, None, None),
        P("prow", "pcol", None, None, None),
    )
    out_specs = (P("prow", "pcol", "zgrid", None, None, None), P("prow", "pcol", None, None, None))
    body = functools.partial(local, nx, (mesh.shape["prow"], mesh.shape["pcol"]))
    return jax.shard_map(body, mesh=mesh, in_specs=in_specs, out_specs=out_specs, check_vma=False)
```
